128 devices in a mesh: req: 16 (over y, x), hid: 8 (over z, core).
Axes of the slice: x: 4, y: 4, z: 4, core: 2. Of those that a mesh axis runs over, the one named last changes fastest.
Arguments:
- tokens: bfloat16 [32, 16, 2, 4096], P('req', 'hid'), may hold values from -6 to 6
- input_gain: float32 [4096], replicated, may hold values from 0.1 to 1.9
- qkv_weight: bfloat16 [4096, 3, 4096], P(None, None, 'hid'), may hold values from -0.09375 to 0.09375
- out_weight: bfloat16 [4096, 4096], P('hid'), may hold values from -0.375 to 0.375
- in_weight: bfloat16 [4096, 16384], P(None, ('req', 'hid')), may hold values from -0.09375 to 0.09375
- down_weight: bfloat16 [16384, 4096], P(('req', 'hid')), may hold values from -0.046875 to 0.046875
- final_gain: float32 [4096], replicated, may hold values from 0.1 to 1.9
- score_weight: bfloat16 [4096], replicated, may hold values from -0.09375 to 0.09375
- prompt_keys: bfloat16 [32, 2048, 4096], P('req', None, 'hid'), may hold values from -260 to 260
- prompt_values: bfloat16 [32, 2048, 4096], P('req', None, 'hid'), may hold values from -6 to 6
- tail_keys: bfloat16 [32, 16, 64, 4096], P('req', None, None, 'hid'), may hold values from -12 to 12
- tail_values: bfloat16 [32, 16, 64, 4096], P('req', None, None, 'hid'), may hold values from -6 to 6
- prompt_lengths: int32 [32], P('req'), may hold values from 1 to 2048
- tail_lengths: int32 [32, 16], P('req'), may hold values from 0 to 64
Outputs:
- next_hidden: bfloat16 [32, 16, 2, 4096], P('req', 'hid')
- sample_scores: float32 [32, 16, 2], P('req', 'hid')
The draws below stay inside these ranges and needn't reach their ends.
Inputs may be any that keep to these rules, and one draw needn't show every extreme that they name: `prompt_lengths`: a request's prompt occupies positions 0 to its length - 1. `tail_lengths`: a sample's tail occupies positions 0 to its length - 1.
All inputs are finite; a program needn't handle non-finite values.
Results may differ from the reference program's by a relative error of at most 0.017.
Values may be sent and summed in bfloat16 or wider, within the bound.
No kernel may reach another device: no remote copies, remote signals or barrier semaphores. Data moves between devices by JAX's collectives and lax.ppermute only.
A program may use at most 128 MiB of HBM per device.

```python
import jax
import jax.numpy as jnp
from jax import lax

D = 4096
HEADS = 16
HEAD_DIM = 256
ROT = 64
FF = 16384
SAMPLES = 16
NEW = 2
PROMPT = 2048
TAIL = 64
REQUESTS = 32
TOKENS = 1024


def draw_prompt_keys(key, part):
    base_key = jax.random.fold_in(key, 0)
    key_dims = (REQUESTS, PROMPT, D)
    drawn = jnp.clip(jax.random.normal(base_key, key_dims, jnp.float32), -6.0, 6.0) * 2.0
    return drawn.astype(jnp.bfloat16)


def set_ends(result, own_key, least, largest):
    shape = result.shape
    spot = [jax.random.randint(jax.random.fold_in(own_key, axis), (), 0, shape[axis]) for axis in range(len(shape))]
    result = result.at[tuple(spot)].set(least)
    longest = shape.index(max(shape))
    spot[longest] = (spot[longest] + 1) % shape[longest]
    return result.at[tuple(spot)].set(largest)


def levels(own_key, extent, cuts, smallest, largest):
    level = 1.0
    for dim, blocks in cuts:
        heights = jax.random.uniform(jax.random.fold_in(jax.random.fold_in(own_key, 6), dim), (blocks,), jnp.float32, smallest / len(cuts), largest / len(cuts))
        level = level * jnp.repeat(jnp.exp(heights), extent[dim] // blocks).reshape((-1,) + (1,) * (len(extent) - 1 - dim))
    return level


def bell_draw(own_key, extent, deviation, most, shards=(), kind=jnp.bfloat16):
    level = levels(own_key, extent, shards, -0.22, 0.18) if shards else 1.0
    entries = jax.random.normal(own_key, extent, jnp.float32) * deviation * level
    return jnp.minimum(jnp.maximum(entries, -most), most).astype(kind)


def setup_inputs(seed: int = 0) -> dict:
    key_list = jax.random.split(jax.random.key(seed), 15)
    tokens = bell_draw(key_list[0], (REQUESTS, SAMPLES, NEW, D), 1.0, 6.0, ((0, 16), (1, 8)))
    input_gain = jnp.clip(1.0 + 0.18 * jax.random.normal(key_list[1], (D,), jnp.float32), 0.1, 1.9)
    qkv_weight = bell_draw(key_list[2], (D, 3, D), D ** -0.5, 0.09375, ((2, 8),))
    out_weight = bell_draw(key_list[3], (D, D), (D // 16) ** -0.5, 0.375, ((0, 8),))
    in_weight = bell_draw(key_list[4], (D, FF), D ** -0.5, 0.09375, ((1, 128),))
    down_weight = bell_draw(key_list[5], (FF, D), FF ** -0.5, 0.046875, ((0, 128),))
    final_gain = jnp.clip(1.0 + 0.18 * jax.random.normal(key_list[6], (D,), jnp.float32), 0.1, 1.9)
    score_weight = bell_draw(key_list[7], (D,), D ** -0.5, 0.09375)
    prompt_keys = draw_prompt_keys(jax.random.fold_in(key_list[14], 71), 0)
    prompt_values = bell_draw(key_list[9], (REQUESTS, PROMPT, D), 1.0, 6.0, ((0, 16), (2, 8)))
    tail_keys = bell_draw(key_list[10], (REQUESTS, SAMPLES, TAIL, D), 2.0, 12.0, ((0, 16), (3, 8)))
    tail_values = bell_draw(key_list[11], (REQUESTS, SAMPLES, TAIL, D), 1.0, 6.0, ((0, 16), (3, 8)))
    prompt_lengths = set_ends(jax.random.randint(key_list[12], (REQUESTS,), 1, PROMPT + 1), jax.random.fold_in(key_list[12], 1), 1, PROMPT).astype(jnp.int32)
    tail_lengths = set_ends(jax.random.randint(key_list[13], (REQUESTS, SAMPLES), 0, TAIL + 1), jax.random.fold_in(key_list[13], 1), 0, TAIL).astype(jnp.int32)
    return dict(tokens=tokens, input_gain=input_gain, qkv_weight=qkv_weight, out_weight=out_weight, in_weight=in_weight, down_weight=down_weight, final_gain=final_gain, score_weight=score_weight, prompt_keys=prompt_keys, prompt_values=prompt_values, tail_keys=tail_keys, tail_values=tail_values, prompt_lengths=prompt_lengths, tail_lengths=tail_lengths)


very_low = -1e+30

def layer_norm(values, gain):
    centre = lax.optimization_barrier(jnp.mean(values, axis=-1, keepdims=True))
    centred = values - centre
    spread = lax.optimization_barrier(jnp.mean(centred * centred, axis=-1, keepdims=True))
    return centred * lax.rsqrt(spread + 1e-05) * gain

def rotate(vectors, positions):
    half_rot = ROT // 2
    frequency = 10000.0 ** (-(jnp.arange(half_rot, dtype=jnp.float32) * (2.0 / ROT)))
    angles = positions.astype(jnp.float32)[..., None] * frequency
    cosine = jnp.cos(angles)[..., None, :]
    sine_part = jnp.sin(angles)[..., None, :]
    paired = vectors[..., :ROT].reshape(vectors.shape[:-1] + (half_rot, 2))
    even_part = paired[..., 0]
    odd_part = paired[..., 1]
    turned = jnp.stack([even_part * cosine - odd_part * sine_part, odd_part * cosine + even_part * sine_part], axis=-1)
    return jnp.concatenate([turned.reshape(vectors.shape[:-1] + (ROT,)), vectors[..., ROT:]], axis=-1)

def widen(array):
    return array.astype(jnp.float32)

def attend_one(operands):
    queries, new_keys, new_values, cached_keys, cached_values, later_keys, later_values, prompt_len, tail_len = operands
    score_scale = HEAD_DIM ** (-0.5)
    prompt_scores = jnp.einsum('sthd,khd->sthk', widen(queries), widen(cached_keys)) * score_scale
    prompt_keep = (jnp.arange(PROMPT, dtype=jnp.int32) < prompt_len)[None, None, None, :]
    tail_scores = jnp.einsum('sthd,skhd->sthk', widen(queries), widen(later_keys)) * score_scale
    tail_keep = (jnp.arange(TAIL, dtype=jnp.int32)[None, :] < tail_len[:, None])[:, None, None, :]
    self_scores = jnp.einsum('sthd,suhd->sthu', widen(queries), widen(new_keys)) * score_scale
    position_order = jnp.arange(NEW, dtype=jnp.int32)
    self_keep = (position_order[None, :] <= position_order[:, None])[None, :, None, :]
    highest = jnp.maximum(lax.optimization_barrier(jnp.max(jnp.where(prompt_keep, prompt_scores, very_low), axis=-1)), lax.optimization_barrier(jnp.max(jnp.where(tail_keep, tail_scores, very_low), axis=-1)))
    highest = jnp.maximum(highest, lax.optimization_barrier(jnp.max(jnp.where(self_keep, self_scores, very_low), axis=-1)))
    prompt_weights = jnp.where(prompt_keep, jnp.exp(prompt_scores - highest[..., None]), 0.0)
    tail_weights = jnp.where(tail_keep, jnp.exp(tail_scores - highest[..., None]), 0.0)
    self_weights = jnp.where(self_keep, jnp.exp(self_scores - highest[..., None]), 0.0)
    totals = lax.optimization_barrier(jnp.sum(prompt_weights, axis=-1)) + lax.optimization_barrier(jnp.sum(tail_weights, axis=-1)) + lax.optimization_barrier(jnp.sum(self_weights, axis=-1))
    accrued = jnp.einsum('sthk,khd->sthd', widen(prompt_weights.astype(jnp.bfloat16)), widen(cached_values))
    accrued = accrued + jnp.einsum('sthk,skhd->sthd', widen(tail_weights.astype(jnp.bfloat16)), widen(later_values))
    accrued = accrued + jnp.einsum('sthu,suhd->sthd', widen(self_weights.astype(jnp.bfloat16)), widen(new_values))
    return (accrued / totals[..., None]).astype(jnp.bfloat16)

def reference(tokens, input_gain, qkv_weight, out_weight, in_weight, down_weight, final_gain, score_weight, prompt_keys, prompt_values, tail_keys, tail_values, prompt_lengths, tail_lengths):
    residual = tokens.astype(jnp.float32).reshape(TOKENS, D)
    normed = layer_norm(residual, input_gain).astype(jnp.bfloat16)
    mixed_qkv = jnp.dot(normed, qkv_weight.reshape(D, 3 * D), preferred_element_type=jnp.float32).astype(jnp.bfloat16)
    mixed_qkv = mixed_qkv.reshape(REQUESTS, SAMPLES, NEW, 3, HEADS, HEAD_DIM)
    positions = prompt_lengths[:, None, None] + tail_lengths[:, :, None] + jnp.arange(NEW, dtype=jnp.int32)[None, None, :]
    queries = rotate(mixed_qkv[:, :, :, 0].astype(jnp.float32), positions).astype(jnp.bfloat16)
    new_keys = rotate(mixed_qkv[:, :, :, 1].astype(jnp.float32), positions).astype(jnp.bfloat16)
    new_values = mixed_qkv[:, :, :, 2]
    cached_keys = prompt_keys.reshape(REQUESTS, PROMPT, HEADS, HEAD_DIM)
    cached_values = prompt_values.reshape(REQUESTS, PROMPT, HEADS, HEAD_DIM)
    later_keys = tail_keys.reshape(REQUESTS, SAMPLES, TAIL, HEADS, HEAD_DIM)
    later_values = tail_values.reshape(REQUESTS, SAMPLES, TAIL, HEADS, HEAD_DIM)
    attended = lax.map(attend_one, (queries, new_keys, new_values, cached_keys, cached_values, later_keys, later_values, prompt_lengths, tail_lengths))
    attended = attended.reshape(TOKENS, D)
    projected = jnp.dot(attended, out_weight, preferred_element_type=jnp.float32)
    hidden_units = jax.nn.gelu(jnp.dot(normed, in_weight, preferred_element_type=jnp.float32), approximate=True).astype(jnp.bfloat16)
    final_state = residual + projected + jnp.dot(hidden_units, down_weight, preferred_element_type=jnp.float32)
    next_hidden = final_state.astype(jnp.bfloat16).reshape(REQUESTS, SAMPLES, NEW, D)
    sample_scores = lax.optimization_barrier(jnp.sum(layer_norm(final_state, final_gain) * score_weight.astype(jnp.float32), axis=-1))
    return (next_hidden, sample_scores.reshape(REQUESTS, SAMPLES, NEW))
```

```python
import jax
import jax.numpy as jnp
from jax import lax
from jax.experimental import pallas as pl
from jax.experimental.pallas import tpu as pltpu
from jax.sharding import Mesh
from jax.sharding import PartitionSpec as P

HEAD_DIM = 256
ROT = 64
VERY_LOW = -1e30
SIDE = 4
CORES = 2
AXES = ("y", "x", "u", "w", "c")
REQ = ("y", "x")
HID = ("u", "w", "c")


def device_at(y, x, z, core):
    return (((y % SIDE) * SIDE + x % SIDE) * SIDE + z % SIDE) * CORES + core


def places():
    for y in range(SIDE):
        for x in range(SIDE):
            for z in range(SIDE):
                for core in range(CORES):
                    yield y, x, z, core


def token_groups():
    groups = {}
    for y, x, z, core in places():
        groups.setdefault(((x + z) % 2, (y + z) % 2, core), []).append(device_at(y, x, z, core))
    return [sorted(group) for group in groups.values()]


def from_neighbour(values, axis):
    moves = []
    for y, x, z, core in places():
        step = 1 - 2 * core
        target = device_at(
            y + step * (axis == "y"), x + step * (axis == "x"), z + step * (axis == "z"), core
        )
        moves.append((device_at(y, x, z, core), target))
    return lax.ppermute(values, AXES, moves)


def swap(values, axis):
    return lax.ppermute(values, axis, [(0, 1), (1, 0)])


def layer_norm(values, gain):
    centre = jnp.mean(values, axis=-1, keepdims=True)
    centred = values - centre
    spread = jnp.mean(centred * centred, axis=-1, keepdims=True)
    return centred * lax.rsqrt(spread + 1e-05) * gain


def rotation_tables(positions):
    half_rot = ROT // 2
    frequency = 10000.0 ** (-(jnp.arange(half_rot, dtype=jnp.float32) * (2.0 / ROT)))
    angles = positions.astype(jnp.float32)[..., None] * jnp.repeat(frequency, 2)
    sign = jnp.where(jnp.arange(ROT) % 2 == 0, -1.0, 1.0)
    rest = [(0, 0)] * (angles.ndim - 1) + [(0, HEAD_DIM - ROT)]
    return (
        jnp.pad(jnp.cos(angles), rest, constant_values=1.0),
        jnp.pad(jnp.sin(angles) * sign, rest),
    )


def qkv_body(rows_ref, weight_ref, out_ref):
    out_ref[0] = jnp.dot(
        rows_ref[...], weight_ref[0], preferred_element_type=jnp.float32
    ).astype(jnp.bfloat16)


def qkv_call(rows, weight):
    count, width = rows.shape
    triple, _, columns = weight.shape
    return pl.pallas_call(
        qkv_body,
        out_shape=jax.ShapeDtypeStruct((triple, count, columns), jnp.bfloat16),
        grid=(triple, columns // HEAD_DIM),
        in_specs=[
            pl.BlockSpec((count, width), lambda i, j: (0, 0)),
            pl.BlockSpec((1, width, HEAD_DIM), lambda i, j: (i, 0, j)),
        ],
        out_specs=pl.BlockSpec((1, count, HEAD_DIM), lambda i, j: (i, 0, j)),
        cost_estimate=pl.CostEstimate(
            flops=2 * count * width * triple * columns,
            bytes_accessed=2 * width * triple * columns,
            transcendentals=0,
        ),
        name="qkv",
    )(rows, weight)


def attention_body(
    meta_ref, qkv_ref, cos_ref, sin_ref, tails_ref, pk_ref, pv_ref, tk_ref, tv_ref, wo_ref, out_ref, acc_ref
):
    head, request = pl.program_id(0), pl.program_id(1)
    prompt_len = meta_ref[request]
    hid = meta_ref[2]
    count = qkv_ref.shape[1]
    here = cos_ref.shape[1]
    row = lax.broadcasted_iota(jnp.int32, (here, count), 0)
    col = lax.broadcasted_iota(jnp.int32, (here, count), 1)
    block = col >> 3
    owner = hid ^ (((block & 1) << 2) | (block & 2) | (block >> 2))
    pick = (((col >> 2) & 1) == request) & (owner == (row >> 2)) & ((col & 3) == (row & 3))
    pick = jnp.where(pick, 1.0, 0.0).astype(jnp.bfloat16)

    def chosen(part):
        return jnp.dot(pick, qkv_ref[part], preferred_element_type=jnp.float32)

    even = lax.broadcasted_iota(jnp.int32, (here, HEAD_DIM), 1) % 2 == 0

    def turned(part):
        values = chosen(part)
        other = jnp.where(
            even, pltpu.roll(values, HEAD_DIM - 1, 1), pltpu.roll(values, 1, 1)
        )
        return (values * cos_ref[0] + other * sin_ref[0]).astype(jnp.bfloat16)

    queries, new_keys = turned(0), turned(1)
    new_values = chosen(2).astype(jnp.bfloat16)
    scale = HEAD_DIM ** (-0.5)

    def scores(keys):
        return (
            lax.dot_general(
                queries, keys, (((1,), (1,)), ((), ())), preferred_element_type=jnp.float32
            )
            * scale
        )

    def places_of(shape):
        return lax.broadcasted_iota(jnp.int32, shape, 0), lax.broadcasted_iota(jnp.int32, shape, 1)

    prompt = scores(pk_ref[0])
    _, at = places_of(prompt.shape)
    prompt = jnp.where(at < prompt_len, prompt, VERY_LOW)
    tail = scores(tk_ref[0])
    line, at = places_of(tail.shape)
    tail_len = tk_ref.shape[1] // (here // 2)
    keep = (at // tail_len == line // 2) & (at % tail_len < tails_ref[0])
    tail = jnp.where(keep, tail, VERY_LOW)
    fresh = scores(new_keys)
    line, at = places_of(fresh.shape)
    fresh = jnp.where((at // 2 == line // 2) & (at <= line), fresh, VERY_LOW)
    top = jnp.maximum(
        jnp.max(prompt, axis=1, keepdims=True),
        jnp.maximum(jnp.max(tail, axis=1, keepdims=True), jnp.max(fresh, axis=1, keepdims=True)),
    )
    total = jnp.zeros((here, 1), jnp.float32)
    summed = jnp.zeros((here, HEAD_DIM), jnp.float32)
    for part, values in ((prompt, pv_ref[0]), (tail, tv_ref[0]), (fresh, new_values)):
        weights = jnp.exp(part - top)
        total = total + jnp.sum(weights, axis=1, keepdims=True)
        summed = summed + jnp.dot(
            weights.astype(jnp.bfloat16), values, preferred_element_type=jnp.float32
        )
    attended = (summed / total).astype(jnp.bfloat16)
    placed = lax.dot_general(
        pick, attended, (((0,), (0,)), ((), ())), preferred_element_type=jnp.float32
    ).astype(jnp.bfloat16)
    term = jnp.dot(placed, wo_ref[...], preferred_element_type=jnp.float32)

    @pl.when((head == 0) & (request == 0))
    def _():
        acc_ref[...] = term

    @pl.when((head > 0) | (request > 0))
    def _():
        acc_ref[...] += term

    @pl.when((head == pl.num_programs(0) - 1) & (request == pl.num_programs(1) - 1))
    def _():
        out_ref[...] = acc_ref[...].astype(jnp.bfloat16)


def attention_call(meta, qkv, cosine, sine, tails, pk, pv, tk, tv, wo):
    triple, count, columns = qkv.shape
    requests, prompt_len, _ = pk.shape
    here = cosine.shape[1]
    width = wo.shape[1]
    keys = prompt_len + tk.shape[1]
    whole = lambda h, r, m: (r, 0, 0)
    cached = lambda h, r, m: (r, 0, h)
    return pl.pallas_call(
        attention_body,
        out_shape=jax.ShapeDtypeStruct((count, width), jnp.bfloat16),
        grid_spec=pltpu.PrefetchScalarGridSpec(
            num_scalar_prefetch=1,
            grid=(columns // HEAD_DIM, requests),
            in_specs=[
                pl.BlockSpec((triple, count, HEAD_DIM), lambda h, r, m: (0, 0, h)),
                pl.BlockSpec((1, here, HEAD_DIM), whole),
                pl.BlockSpec((1, here, HEAD_DIM), whole),
                pl.BlockSpec((1, here, 1), whole),
                pl.BlockSpec((1, prompt_len, HEAD_DIM), cached),
                pl.BlockSpec((1, prompt_len, HEAD_DIM), cached),
                pl.BlockSpec((1, tk.shape[1], HEAD_DIM), cached),
                pl.BlockSpec((1, tk.shape[1], HEAD_DIM), cached),
                pl.BlockSpec((HEAD_DIM, width), lambda h, r, m: (h, 0)),
            ],
            out_specs=pl.BlockSpec((count, width), lambda h, r, m: (0, 0)),
            scratch_shapes=[pltpu.VMEM((count, width), jnp.float32)],
        ),
        cost_estimate=pl.CostEstimate(
            flops=4 * requests * here * keys * columns + 2 * count * columns * width,
            bytes_accessed=4 * requests * keys * columns + 2 * columns * width,
            transcendentals=requests * here * keys * (columns // HEAD_DIM),
        ),
        name="attention",
    )(meta, qkv, cosine, sine, tails, pk, pv, tk, tv, wo)


MLP_STEPS = 4


def mlp_body(*refs):
    t_own, t_other = refs[:2]
    ups, downs = refs[2:6], refs[6:10]
    o_own, o_other, acc_ref, hidden_ref = refs[10:]
    step = pl.program_id(0)

    @pl.when(step < MLP_STEPS)
    def _():
        rows = jnp.concatenate([t_own[...], t_other[...]], axis=0)
        term = jnp.dot(
            rows, jnp.concatenate([up[...] for up in ups], axis=1), preferred_element_type=jnp.float32
        )

        @pl.when(step == 0)
        def _():
            acc_ref[...] = term

        @pl.when(step > 0)
        def _():
            acc_ref[...] += term

    @pl.when(step == MLP_STEPS - 1)
    def _():
        hidden_ref[...] = jax.nn.gelu(acc_ref[...], approximate=True).astype(jnp.bfloat16)

    @pl.when(step >= MLP_STEPS)
    def _():
        result = jnp.dot(
            hidden_ref[...],
            jnp.concatenate([down[...] for down in downs], axis=0),
            preferred_element_type=jnp.float32,
        ).astype(jnp.bfloat16)
        half = result.shape[0] // 2
        o_own[...] = result[:half]
        o_other[...] = result[half:]


def mlp_call(t_own, t_other, ups, downs):
    count, width = t_own.shape
    units = ups[0].shape[1]
    chunk = width // MLP_STEPS
    first = lambda i: jnp.minimum(i, MLP_STEPS - 1)
    second = lambda i: jnp.maximum(i - MLP_STEPS, 0)
    rows = pl.BlockSpec((count, chunk), lambda i: (0, first(i)))
    out = pl.BlockSpec((count, chunk), lambda i: (0, second(i)))
    return pl.pallas_call(
        mlp_body,
        out_shape=[jax.ShapeDtypeStruct((count, width), jnp.bfloat16)] * 2,
        grid=(2 * MLP_STEPS,),
        in_specs=[rows, rows]
        + [pl.BlockSpec((chunk, units), lambda i: (first(i), 0))] * 4
        + [pl.BlockSpec((units, chunk), lambda i: (0, second(i)))] * 4,
        out_specs=[out, out],
        scratch_shapes=[
            pltpu.VMEM((2 * count, 4 * units), jnp.float32),
            pltpu.VMEM((2 * count, 4 * units), jnp.bfloat16),
        ],
        cost_estimate=pl.CostEstimate(
            flops=4 * 2 * count * width * 4 * units,
            bytes_accessed=2 * (4 * count * width + 8 * units * width),
            transcendentals=2 * count * 4 * units,
        ),
        name="mlp",
    )(t_own, t_other, *ups, *downs)


def shards(
    tokens,
    input_gain,
    qkv_weight,
    out_weight,
    in_weight,
    down_weight,
    final_gain,
    score_weight,
    prompt_keys,
    prompt_values,
    tail_keys,
    tail_values,
    prompt_lengths,
    tail_lengths,
):
    req_dev, samp_dev, fresh, width = tokens.shape
    own_rows = req_dev * samp_dev * fresh
    ups = [in_weight] + [from_neighbour(in_weight, axis) for axis in "xyz"]
    downs = [down_weight] + [from_neighbour(down_weight, axis) for axis in "xyz"]
    residual = tokens.astype(jnp.float32).reshape(own_rows, width)
    normed = layer_norm(residual, input_gain).astype(jnp.bfloat16)
    groups = token_groups()
    sharing = len(groups[0])
    visitors = lax.all_to_all(
        jnp.tile(normed, (sharing, 1)), AXES, 0, 0, axis_index_groups=groups, tiled=True
    )

    rows = normed
    for axis in HID:
        rows = jnp.concatenate([rows, swap(rows, axis)], axis=0)
    qkv = qkv_call(rows, jnp.transpose(qkv_weight, (1, 0, 2)))
    positions = (
        prompt_lengths[:, None, None]
        + tail_lengths[:, :, None]
        + jnp.arange(fresh, dtype=jnp.int32)[None, None, :]
    )
    samples = tail_lengths.shape[1]
    cosine, sine = rotation_tables(positions.reshape(req_dev, samples * fresh))
    tails = jnp.repeat(tail_lengths, fresh, axis=1)[:, :, None]
    meta = jnp.concatenate([prompt_lengths, lax.axis_index(HID).astype(jnp.int32)[None]])
    slab = tail_keys.shape[-1]
    partial = attention_call(
        meta,
        qkv,
        cosine,
        sine,
        tails,
        prompt_keys,
        prompt_values,
        tail_keys.reshape(req_dev, -1, slab),
        tail_values.reshape(req_dev, -1, slab),
        out_weight,
    )
    for axis in reversed(HID):
        half = partial.shape[0] // 2
        partial = partial[:half].astype(jnp.float32) + swap(partial[half:], axis).astype(jnp.float32)
        if axis != HID[0]:
            partial = partial.astype(jnp.bfloat16)

    mine, others = mlp_call(visitors, swap(visitors, "c"), ups, downs)
    summed = mine.astype(jnp.float32) + swap(others, "c").astype(jnp.float32)
    returned = lax.all_to_all(
        summed.astype(jnp.bfloat16), AXES, 0, 0, axis_index_groups=groups, tiled=True
    )
    feed_forward = jnp.sum(
        returned.reshape(sharing, own_rows, width).astype(jnp.float32), axis=0
    )

    final_state = residual + partial + feed_forward
    next_hidden = final_state.astype(jnp.bfloat16).reshape(req_dev, samp_dev, fresh, width)
    sample_scores = jnp.sum(
        layer_norm(final_state, final_gain) * score_weight.astype(jnp.float32), axis=-1
    )
    return (next_hidden, sample_scores.reshape(req_dev, samp_dev, fresh))


def solution(mesh):
    grid = Mesh(mesh.devices.reshape(SIDE, SIDE, 2, 2, CORES), AXES)
    placed = (
        P(REQ, HID, None, None),
        P(),
        P(None, None, HID),
        P(HID, None),
        P(None, REQ + HID),
        P(REQ + HID, None),
        P(),
        P(),
        P(REQ, None, HID),
        P(REQ, None, HID),
        P(REQ, None, None, HID),
        P(REQ, None, None, HID),
        P(REQ),
        P(REQ, None),
    )
    return jax.shard_map(
        shards,
        mesh=grid,
        in_specs=placed,
        out_specs=(P(REQ, HID, None, None), P(REQ, HID, None)),
        check_vma=False,
    )
```

```python
import jax
import jax.numpy as jnp
from jax import lax
from jax.experimental import pallas as pl
from jax.experimental.pallas import tpu as pltpu
from jax.sharding import Mesh
from jax.sharding import PartitionSpec as P

HEAD_DIM = 256
ROT = 64
LANES = 128
VERY_LOW = -1e30
CUT = 2
MIB = 2**20
SMEM = pl.BlockSpec(memory_space=pltpu.SMEM)
VMEM = pl.BlockSpec(memory_space=pltpu.VMEM)
HBM = pl.BlockSpec(memory_space=pltpu.HBM)
SIDE = 4
CORES = 2
AXES = ("y", "x", "u", "w", "c")
REQ = ("y", "x")
HID = ("u", "w", "c")


def device_at(y, x, z, core):
    return (((y % SIDE) * SIDE + x % SIDE) * SIDE + z % SIDE) * CORES + core


def places():
    for y in range(SIDE):
        for x in range(SIDE):
            for z in range(SIDE):
                for core in range(CORES):
                    yield y, x, z, core


def token_groups():
    groups = {}
    for y, x, z, core in places():
        groups.setdefault(((x + z) % 2, (y + z) % 2, core), []).append(device_at(y, x, z, core))
    return [sorted(group) for group in groups.values()]


def from_neighbour(values, axis):
    moves = []
    for y, x, z, core in places():
        step = 1 - 2 * core
        target = device_at(
            y + step * (axis == "y"), x + step * (axis == "x"), z + step * (axis == "z"), core
        )
        moves.append((device_at(y, x, z, core), target))
    return lax.ppermute(values, AXES, moves)


def swap(values, *axes):
    last = 2 ** len(axes) - 1
    return lax.ppermute(values, axes, [(i, last - i) for i in range(last + 1)])


def normalised(values, gain):
    centred = values - jnp.mean(values, axis=1, keepdims=True)
    spread = jnp.mean(centred * centred, axis=1, keepdims=True)
    return centred * lax.rsqrt(spread + 1e-05) * gain


def start_body(
    tokens_hbm, gain_hbm, up_hbm, down_hbm, normed_ref, copies_ref, packed_hbm, tokens_ref, gain_ref, rows, packed, down_ref, sem, out_sem
):
    requests, samples, fresh, width = tokens_ref.shape
    blocks = up_hbm.shape[0]
    upper, lower = pl.ds(0, blocks), pl.ds(blocks, blocks)
    inward = [
        pltpu.make_async_copy(down_hbm, down_ref, sem.at[0]),
        pltpu.make_async_copy(up_hbm, packed.at[upper], sem.at[1]),
        pltpu.make_async_copy(tokens_hbm, tokens_ref, sem.at[2]),
        pltpu.make_async_copy(gain_hbm, gain_ref, sem.at[3]),
    ]
    outward = [
        pltpu.make_async_copy(packed.at[lower], packed_hbm.at[lower], out_sem.at[0]),
        pltpu.make_async_copy(packed.at[upper], packed_hbm.at[upper], out_sem.at[1]),
    ]
    for copy in inward:
        copy.start()
    inward[0].wait()
    for j in range(blocks):
        packed[blocks + j] = down_ref[:, j * LANES : (j + 1) * LANES]
    outward[0].start()
    inward[1].wait()
    outward[1].start()
    inward[2].wait()
    inward[3].wait()
    for r in range(requests):
        for s in range(samples):
            at = (r * samples + s) * fresh
            rows[at : at + fresh] = tokens_ref[r, s].astype(jnp.float32)
    normed = normalised(rows[...], gain_ref[...]).astype(jnp.bfloat16)
    normed_ref[...] = normed
    for i in range(copies_ref.shape[0]):
        copies_ref[i] = normed
    for copy in outward:
        copy.wait()


def start_call(tokens, gain, up, down, sharing):
    requests, samples, fresh, width = tokens.shape
    own_rows = requests * samples * fresh
    blocks = width // LANES
    return pl.pallas_call(
        start_body,
        out_shape=[
            jax.ShapeDtypeStruct((own_rows, width), jnp.bfloat16),
            jax.ShapeDtypeStruct((sharing, own_rows, width), jnp.bfloat16),
            jax.ShapeDtypeStruct((2 * blocks, LANES, LANES), jnp.bfloat16),
        ],
        in_specs=[HBM] * 4,
        out_specs=[VMEM, VMEM, HBM],
        scratch_shapes=[
            pltpu.VMEM(tokens.shape, jnp.bfloat16),
            pltpu.VMEM((1, width), jnp.float32),
            pltpu.VMEM((own_rows, width), jnp.float32),
            pltpu.VMEM((2 * blocks, LANES, LANES), jnp.bfloat16),
            pltpu.VMEM(down.shape, jnp.bfloat16),
            pltpu.SemaphoreType.DMA((4,)),
            pltpu.SemaphoreType.DMA((2,)),
        ],
        compiler_params=pltpu.CompilerParams(vmem_limit_bytes=60 * MIB),
        name="start",
    )(tokens, gain.reshape(1, width), up.reshape(blocks, LANES, LANES), down)


def iotas(shape):
    return lax.broadcasted_iota(jnp.int32, shape, 0), lax.broadcasted_iota(jnp.int32, shape, 1)

def mixer_body(
    plen_ref, tlen_ref, hid_ref, near_ref, far_ref, turn_ref, wq_hbm, pk_hbm, pv_hbm, tk_hbm, tv_hbm, wo_hbm,
    out_ref, wq, pk, pv, tk, tv, wo, wq_sem, cache_sem, wo_sem
):
    parts, width, columns = wq.shape
    requests, prompt_len, _ = pk.shape
    samples = tlen_ref.shape[1]
    tail_len = tk.shape[1] // samples
    count = near_ref.shape[0] + far_ref.shape[0]
    here = count // requests
    fresh = here // samples
    heads = columns // HEAD_DIM
    slab = width // CUT
    def wq_copy(t, k):
        rows = pl.ds(k * slab, slab)
        return pltpu.make_async_copy(wq_hbm.at[t, rows], wq.at[t, rows], wq_sem.at[t, k])
    caches = ((pk_hbm, pk), (tk_hbm, tk), (pv_hbm, pv), (tv_hbm, tv))
    def cache_copy(r, i):
        source, target = caches[i]
        return pltpu.make_async_copy(source.at[r], target.at[r], cache_sem.at[r, i])
    def wo_copy(h):
        rows = pl.ds(h * HEAD_DIM, HEAD_DIM)
        return pltpu.make_async_copy(wo_hbm.at[rows], wo.at[rows], wo_sem.at[h])
    for t in range(parts):
        for k in range(CUT):
            wq_copy(t, k).start()
    for r in range(requests):
        for i in range(len(caches)):
            cache_copy(r, i).start()
    for h in range(heads):
        wo_copy(h).start()

    rows = jnp.concatenate([near_ref[...], far_ref[...]], axis=0)
    mixed = []
    for t in range(parts):
        acc = None
        for k in range(CUT):
            wq_copy(t, k).wait()
            term = jnp.dot(
                rows[:, k * slab : (k + 1) * slab], wq[t, k * slab : (k + 1) * slab], preferred_element_type=jnp.float32
            )
            acc = term if acc is None else acc + term
        mixed.append(acc.astype(jnp.bfloat16))

    row, col = iotas((count, count))
    block = col >> 3
    owner = hid_ref[0] ^ (((block & 1) << 2) | (block & 2) | (block >> 2))
    pick = (((col >> 2) & 1) == row // here) & (owner == ((row % here) >> 2)) & ((col & 3) == (row & 3))
    pick = jnp.where(pick, 1.0, 0.0).astype(jnp.bfloat16)
    ordered = [jnp.dot(pick, part, preferred_element_type=jnp.float32) for part in mixed]
    _, lane = iotas((count, LANES))
    even = lane % 2 == 0
    cosine, sine = turn_ref[0], turn_ref[1]

    def turned(values, h):
        head = values[:, h * HEAD_DIM : h * HEAD_DIM + LANES]
        other = jnp.where(even, pltpu.roll(head, LANES - 1, 1), pltpu.roll(head, 1, 1))
        rest = values[:, h * HEAD_DIM + LANES : (h + 1) * HEAD_DIM]
        return jnp.concatenate([head * cosine + other * sine, rest], axis=1).astype(jnp.bfloat16)

    queries = [turned(ordered[0], h) for h in range(heads)]
    new_keys = [turned(ordered[1], h) for h in range(heads)]
    new_values = ordered[2].astype(jnp.bfloat16)
    scale = HEAD_DIM ** (-0.5)
    line, at = iotas((here, prompt_len))
    tail_line, tail_at = iotas((here, samples * tail_len))
    fresh_line, fresh_at = iotas((here, here))
    fresh_keep = (fresh_at // fresh == fresh_line // fresh) & (fresh_at <= fresh_line)
    sample, _ = iotas((here, 1))
    attended = [[None] * requests for _ in range(heads)]
    for r in range(requests):
        lengths = jnp.zeros((here, 1), jnp.int32)
        for s in range(samples):
            lengths = jnp.where(sample // fresh == s, tlen_ref[r, s], lengths)
        keep = at < plen_ref[r]
        tail_keep = (tail_at // tail_len == tail_line // fresh) & (tail_at % tail_len < lengths)
        own = slice(r * here, (r + 1) * here)
        for i in range(2):
            cache_copy(r, i).wait()
        weighted = []
        for h in range(heads):
            cols = slice(h * HEAD_DIM, (h + 1) * HEAD_DIM)
            query = queries[h][own]
            def scores(keys):
                return lax.dot_general(query, keys, (((1,), (1,)), ((), ())), preferred_element_type=jnp.float32) * scale
            prompt = jnp.where(keep, scores(pk[r, :, cols]), VERY_LOW)
            tail = jnp.where(tail_keep, scores(tk[r, :, cols]), VERY_LOW)
            new = jnp.where(fresh_keep, scores(new_keys[h][own]), VERY_LOW)
            top = jnp.maximum(
                jnp.max(prompt, axis=1, keepdims=True),
                jnp.maximum(jnp.max(tail, axis=1, keepdims=True), jnp.max(new, axis=1, keepdims=True)),
            )
            weights = [jnp.exp(part - top) for part in (prompt, tail, new)]
            total = sum(jnp.sum(part, axis=1, keepdims=True) for part in weights)
            weighted.append(([part.astype(jnp.bfloat16) for part in weights], total))
        for i in range(2, 4):
            cache_copy(r, i).wait()
        for h in range(heads):
            cols = slice(h * HEAD_DIM, (h + 1) * HEAD_DIM)
            weights, total = weighted[h]
            summed = jnp.dot(weights[0], pv[r, :, cols], preferred_element_type=jnp.float32)
            summed = summed + jnp.dot(weights[1], tv[r, :, cols], preferred_element_type=jnp.float32)
            summed = summed + jnp.dot(weights[2], new_values[own, cols], preferred_element_type=jnp.float32)
            attended[h][r] = (summed / total).astype(jnp.bfloat16)
    joined = jnp.concatenate([jnp.concatenate(part, axis=0) for part in attended], axis=1)
    placed = lax.dot_general(pick, joined, (((0,), (0,)), ((), ())), preferred_element_type=jnp.float32).astype(jnp.bfloat16)
    for h in range(heads):
        wo_copy(h).wait()
    out_ref[...] = jnp.dot(placed, wo[...], preferred_element_type=jnp.float32).astype(jnp.bfloat16)


def mixer_call(plen, tlen, hid, near, far, turn, wq, pk, pv, tk, tv, wo):
    parts, width, columns = wq.shape
    requests, prompt_len, _ = pk.shape
    count = near.shape[0] + far.shape[0]
    keys = prompt_len + tk.shape[1]
    return pl.pallas_call(
        mixer_body,
        out_shape=jax.ShapeDtypeStruct((count, width), jnp.bfloat16),
        in_specs=[SMEM] * 3 + [VMEM] * 3 + [HBM] * 6,
        out_specs=VMEM,
        scratch_shapes=[pltpu.VMEM(a.shape, jnp.bfloat16) for a in (wq, pk, pv, tk, tv, wo)]
        + [
            pltpu.SemaphoreType.DMA((parts, CUT)),
            pltpu.SemaphoreType.DMA((requests, 4)),
            pltpu.SemaphoreType.DMA((columns // HEAD_DIM,)),
        ],
        compiler_params=pltpu.CompilerParams(vmem_limit_bytes=60 * MIB),
        cost_estimate=pl.CostEstimate(
            flops=2 * count * columns * (parts * width + 2 * keys + width),
            bytes_accessed=2 * columns * (parts * width + 2 * requests * keys + width),
            transcendentals=count * keys * (columns // HEAD_DIM),
        ),
        name="mixer",
    )(plen, tlen, hid, near, far, turn, wq, pk, pv, tk, tv, wo)


def mlp_body(place_ref, own_ref, other_ref, near_ref, far_ref, *refs):
    packed, (out_own, out_other), (ups, downs, up_sem, down_sem) = refs[:4], refs[4:6], refs[6:]
    blocks = ups.shape[0]
    def up_copy(p):
        return pltpu.make_async_copy(
            packed[p].at[pl.ds(0, blocks)], ups.at[:, :, pl.ds(p * LANES, LANES)], up_sem.at[p]
        )
    def down_copy(p):
        return pltpu.make_async_copy(
            packed[p].at[pl.ds(blocks, blocks)], downs.at[:, pl.ds(p * LANES, LANES), :], down_sem.at[p]
        )
    for p in range(4):
        up_copy(p).start()
    for p in range(4):
        down_copy(p).start()
    rows = jnp.concatenate([own_ref[...], other_ref[...]], axis=0)
    units = ups.shape[2]
    for p in range(4):
        up_copy(p).wait()
    hidden = jnp.dot(rows, ups[...].reshape(blocks * LANES, units), preferred_element_type=jnp.float32)
    hidden = jax.nn.gelu(hidden, approximate=True).astype(jnp.bfloat16)
    for p in range(4):
        down_copy(p).wait()
    half = own_ref.shape[0]
    for j in range(0, blocks, 2):
        result = jnp.dot(
            hidden, jnp.concatenate([downs[j], downs[j + 1]], axis=1), preferred_element_type=jnp.float32
        ).astype(jnp.bfloat16)
        cols = slice(j * LANES, (j + 2) * LANES)
        out_own[:, cols] = result[:half]
        out_other[:, cols] = result[half:]
    count = near_ref.shape[0] // 2
    for i in range(2):
        at = pl.ds(pl.multiple_of((place_ref[0] ^ i) * count, count), count)
        part = pl.ds(i * count, count)
        out_own[at] = (
            out_own[at].astype(jnp.float32)
            + near_ref[part].astype(jnp.float32)
            + far_ref[part].astype(jnp.float32)
        ).astype(jnp.bfloat16)


def mlp_call(place, own, other, near, far, packed):
    count, width = own.shape
    units = 4 * LANES
    blocks = width // LANES
    return pl.pallas_call(
        mlp_body,
        out_shape=[jax.ShapeDtypeStruct((count, width), jnp.bfloat16)] * 2,
        in_specs=[SMEM] + [VMEM] * 4 + [HBM] * 4,
        out_specs=[VMEM] * 2,
        scratch_shapes=[
            pltpu.VMEM((blocks, LANES, units), jnp.bfloat16),
            pltpu.VMEM((blocks, units, LANES), jnp.bfloat16),
            pltpu.SemaphoreType.DMA((4,)),
            pltpu.SemaphoreType.DMA((4,)),
        ],
        compiler_params=pltpu.CompilerParams(vmem_limit_bytes=24 * MIB),
        cost_estimate=pl.CostEstimate(
            flops=8 * count * width * units,
            bytes_accessed=2 * (4 * count * width + 2 * units * width),
            transcendentals=2 * count * units,
        ),
        name="mlp",
    )(place, own, other, near, far, *packed)


def add_body(a_ref, b_ref, out_ref):
    out_ref[...] = (a_ref[...].astype(jnp.float32) + b_ref[...].astype(jnp.float32)).astype(jnp.bfloat16)


def add_call(a, b):
    return pl.pallas_call(
        add_body,
        out_shape=jax.ShapeDtypeStruct(b.shape, jnp.bfloat16),
        in_specs=[VMEM] * 2,
        out_specs=VMEM,
        compiler_params=pltpu.CompilerParams(vmem_limit_bytes=8 * MIB),
        name="add",
    )(a, b)


def end_body(tokens_ref, returned_ref, gain_ref, score_ref, next_ref, out_ref, rows):
    requests, samples, fresh, width = tokens_ref.shape
    for r in range(requests):
        for s in range(samples):
            at = (r * samples + s) * fresh
            rows[at : at + fresh] = tokens_ref[r, s].astype(jnp.float32)
    added = returned_ref[0].astype(jnp.float32)
    for i in range(1, returned_ref.shape[0]):
        added = added + returned_ref[i].astype(jnp.float32)
    final = rows[...] + added
    scores = jnp.sum(
        normalised(final, gain_ref[...]) * score_ref[...].astype(jnp.float32), axis=1, keepdims=True
    )
    rows[...] = final
    row, col = iotas((final.shape[0], fresh))
    for r in range(requests):
        for s in range(samples):
            at = (r * samples + s) * fresh
            next_ref[r, s] = rows[at : at + fresh].astype(jnp.bfloat16)
            out_ref[r, s : s + 1] = jnp.sum(jnp.where(row == at + col, scores, 0.0), axis=0, keepdims=True)


def end_call(tokens, returned, gain, score_weight):
    width = tokens.shape[-1]
    return pl.pallas_call(
        end_body,
        out_shape=[
            jax.ShapeDtypeStruct(tokens.shape, jnp.bfloat16),
            jax.ShapeDtypeStruct(tokens.shape[:-1], jnp.float32),
        ],
        in_specs=[VMEM] * 4,
        out_specs=[VMEM] * 2,
        scratch_shapes=[pltpu.VMEM((returned.shape[1], width), jnp.float32)],
        compiler_params=pltpu.CompilerParams(vmem_limit_bytes=8 * MIB),
        name="end",
    )(tokens, returned, gain.reshape(1, width), score_weight.reshape(1, width))


def rotation_tables(positions):
    lane = jnp.arange(LANES, dtype=jnp.int32)
    frequency = 10000.0 ** (-((lane // 2).astype(jnp.float32) * (2.0 / ROT)))
    angles = positions.astype(jnp.float32)[:, None] * frequency
    sign = jnp.where(lane % 2 == 0, -1.0, 1.0)
    rotated = lane < ROT
    return jnp.stack(
        [jnp.where(rotated, jnp.cos(angles), 1.0), jnp.where(rotated, jnp.sin(angles) * sign, 0.0)]
    )


def shards(
    tokens,
    input_gain,
    qkv_weight,
    out_weight,
    in_weight,
    down_weight,
    final_gain,
    score_weight,
    prompt_keys,
    prompt_values,
    tail_keys,
    tail_values,
    prompt_lengths,
    tail_lengths,
):
    req_dev, samp_dev, fresh, width = tokens.shape
    own_rows = req_dev * samp_dev * fresh
    groups = token_groups()
    sharing = len(groups[0])
    normed, copies, own_weights = start_call(tokens, input_gain, in_weight, down_weight, sharing)

    near = jnp.concatenate([normed, swap(normed, "u"), swap(normed, "w"), swap(normed, "u", "w")], axis=0)
    near, late_weights = lax.optimization_barrier((near, own_weights))
    far = swap(near, "c")
    packed = [own_weights] + [from_neighbour(late_weights, axis) for axis in "xyz"]

    def exchange(values):
        return lax.all_to_all(values, AXES, 0, 0, axis_index_groups=groups, tiled=True)

    visitors = exchange(copies).reshape(sharing * own_rows, width)
    positions = (
        prompt_lengths[:, None, None]
        + tail_lengths[:, :, None]
        + jnp.arange(fresh, dtype=jnp.int32)[None, None, :]
    )
    slab = tail_keys.shape[-1]
    partial = mixer_call(
        prompt_lengths,
        tail_lengths,
        lax.axis_index(HID).astype(jnp.int32).reshape(1),
        near,
        far,
        rotation_tables(positions.reshape(-1)),
        jnp.transpose(qkv_weight, (1, 0, 2)),
        prompt_keys,
        prompt_values,
        tail_keys.reshape(req_dev, -1, slab),
        tail_values.reshape(req_dev, -1, slab),
        out_weight,
    )
    other_visitors = swap(visitors, "c")
    half = partial.shape[0] // 2
    projected = add_call(partial[:half], swap(partial[half:], "c"))
    half = projected.shape[0] // 2
    projected_far = swap(projected[half:], "w")
    projected, projected_far, packed, visitors, other_visitors = lax.optimization_barrier(
        (projected, projected_far, packed, visitors, other_visitors)
    )

    place = lax.axis_index("y") * SIDE + lax.axis_index("x") // 2 * 2 + lax.axis_index("u")
    place = place.astype(jnp.int32).reshape(1)
    mine, others = mlp_call(place, visitors, other_visitors, projected[:half], projected_far, packed)
    summed = add_call(mine, swap(others, "c"))
    returned = exchange(summed.reshape(sharing, own_rows, width))
    next_hidden, sample_scores = end_call(tokens, returned, final_gain, score_weight)
    return (next_hidden, sample_scores)


def solution(mesh):
    grid = Mesh(mesh.devices.reshape(SIDE, SIDE, 2, 2, CORES), AXES)
    placed = (
        P(REQ, HID, None, None),
        P(),
        P(None, None, HID),
        P(HID, None),
        P(None, REQ + HID),
        P(REQ + HID, None),
        P(),
        P(),
        P(REQ, None, HID),
        P(REQ, None, HID),
        P(REQ, None, None, HID),
        P(REQ, None, None, HID),
        P(REQ),
        P(REQ, None),
    )
    return jax.shard_map(
        shards,
        mesh=grid,
        in_specs=placed,
        out_specs=(P(REQ, HID, None, None), P(REQ, HID, None)),
        check_vma=False,
    )
```

```python
import jax
import jax.numpy as jnp
from jax import lax
from jax.experimental import pallas as pl
from jax.experimental.pallas import tpu as pltpu
from jax.sharding import Mesh
from jax.sharding import PartitionSpec as P

HEAD_DIM = 256
ROT = 64
LANES = 128
VERY_LOW = -1e30
CUT = 2
MIB = 2**20
SMEM = pl.BlockSpec(memory_space=pltpu.SMEM)
VMEM = pl.BlockSpec(memory_space=pltpu.VMEM)
HBM = pl.BlockSpec(memory_space=pltpu.HBM)
SIDE = 4
CORES = 2
AXES = ("y", "x", "u", "w", "c")
REQ = ("y", "x")
HID = ("u", "w", "c")


def device_at(y, x, z, core):
    return (((y % SIDE) * SIDE + x % SIDE) * SIDE + z % SIDE) * CORES + core


def places():
    for y in range(SIDE):
        for x in range(SIDE):
            for z in range(SIDE):
                for core in range(CORES):
                    yield y, x, z, core


def token_groups():
    groups = {}
    for y, x, z, core in places():
        groups.setdefault(((x + z) % 2, (y + z) % 2, core), []).append(device_at(y, x, z, core))
    return [sorted(group) for group in groups.values()]


def from_neighbour(values, axis):
    moves = []
    for y, x, z, core in places():
        step = 1 - 2 * core
        target = device_at(
            y + step * (axis == "y"), x + step * (axis == "x"), z + step * (axis == "z"), core
        )
        moves.append((device_at(y, x, z, core), target))
    return lax.ppermute(values, AXES, moves)


def swap(values, *axes):
    last = 2 ** len(axes) - 1
    return lax.ppermute(values, axes, [(i, last - i) for i in range(last + 1)])


def normalised(values, gain):
    centred = values - jnp.mean(values, axis=1, keepdims=True)
    spread = jnp.mean(centred * centred, axis=1, keepdims=True)
    return centred * lax.rsqrt(spread + 1e-05) * gain


def start_body(
    tokens_hbm, gain_hbm, up_hbm, down_hbm, normed_ref, copies_hbm, packed_hbm, tokens_ref, gain_ref, rows, packed, down_ref, sem, out_sem, copy_sem
):
    requests, samples, fresh, width = tokens_ref.shape
    blocks = up_hbm.shape[0]
    upper, lower = pl.ds(0, blocks), pl.ds(blocks, blocks)
    inward = [
        pltpu.make_async_copy(tokens_hbm, tokens_ref, sem.at[0]),
        pltpu.make_async_copy(gain_hbm, gain_ref, sem.at[1]),
        pltpu.make_async_copy(down_hbm, down_ref, sem.at[2]),
        pltpu.make_async_copy(up_hbm, packed.at[upper], sem.at[3]),
    ]
    outward = [
        pltpu.make_async_copy(packed.at[lower], packed_hbm.at[lower], out_sem.at[0]),
        pltpu.make_async_copy(packed.at[upper], packed_hbm.at[upper], out_sem.at[1]),
    ]
    copies = [
        pltpu.make_async_copy(normed_ref, copies_hbm.at[i], copy_sem.at[i]) for i in range(copies_hbm.shape[0])
    ]
    for copy in inward:
        copy.start()
    inward[0].wait()
    inward[1].wait()
    for r in range(requests):
        for s in range(samples):
            at = (r * samples + s) * fresh
            rows[at : at + fresh] = tokens_ref[r, s].astype(jnp.float32)
    normed_ref[...] = normalised(rows[...], gain_ref[...]).astype(jnp.bfloat16)
    for copy in copies:
        copy.start()
    inward[2].wait()
    for j in range(blocks):
        packed[blocks + j] = down_ref[:, j * LANES : (j + 1) * LANES]
    outward[0].start()
    inward[3].wait()
    outward[1].start()
    for copy in outward + copies:
        copy.wait()


def start_call(tokens, gain, up, down, sharing):
    requests, samples, fresh, width = tokens.shape
    own_rows = requests * samples * fresh
    blocks = width // LANES
    return pl.pallas_call(
        start_body,
        out_shape=[
            jax.ShapeDtypeStruct((own_rows, width), jnp.bfloat16),
            jax.ShapeDtypeStruct((sharing, own_rows, width), jnp.bfloat16),
            jax.ShapeDtypeStruct((2 * blocks, LANES, LANES), jnp.bfloat16),
        ],
        in_specs=[HBM] * 4,
        out_specs=[VMEM, HBM, HBM],
        scratch_shapes=[
            pltpu.VMEM(tokens.shape, jnp.bfloat16),
            pltpu.VMEM((1, width), jnp.float32),
            pltpu.VMEM((own_rows, width), jnp.float32),
            pltpu.VMEM((2 * blocks, LANES, LANES), jnp.bfloat16),
            pltpu.VMEM(down.shape, jnp.bfloat16),
            pltpu.SemaphoreType.DMA((4,)),
            pltpu.SemaphoreType.DMA((2,)),
            pltpu.SemaphoreType.DMA((sharing,)),
        ],
        compiler_params=pltpu.CompilerParams(vmem_limit_bytes=60 * MIB),
        name="start",
    )(tokens, gain.reshape(1, width), up.reshape(blocks, LANES, LANES), down)


def iotas(shape):
    return lax.broadcasted_iota(jnp.int32, shape, 0), lax.broadcasted_iota(jnp.int32, shape, 1)

def mixer_body(
    plen_ref, tlen_ref, hid_ref, near_ref, far_ref, turn_ref, wq_hbm, pk_hbm, pv_hbm, tk_hbm, tv_hbm, wo_hbm,
    out_ref, wq, pk, pv, tk, tv, wo, wq_sem, cache_sem, wo_sem
):
    parts, width, columns = wq.shape
    requests, prompt_len, _ = pk.shape
    samples = tlen_ref.shape[1]
    tail_len = tk.shape[1] // samples
    count = near_ref.shape[0] + far_ref.shape[0]
    here = count // requests
    fresh = here // samples
    heads = columns // HEAD_DIM
    slab = width // CUT
    def wq_copy(t, k):
        rows = pl.ds(k * slab, slab)
        return pltpu.make_async_copy(wq_hbm.at[t, rows], wq.at[t, rows], wq_sem.at[t, k])
    caches = ((pk_hbm, pk), (tk_hbm, tk), (pv_hbm, pv), (tv_hbm, tv))
    def cache_copy(r, i):
        source, target = caches[i]
        return pltpu.make_async_copy(source.at[r], target.at[r], cache_sem.at[r, i])
    def wo_copy(h):
        rows = pl.ds(h * HEAD_DIM, HEAD_DIM)
        return pltpu.make_async_copy(wo_hbm.at[rows], wo.at[rows], wo_sem.at[h])
    for t in range(parts):
        for k in range(CUT):
            wq_copy(t, k).start()
    for r in range(requests):
        for i in range(len(caches)):
            cache_copy(r, i).start()
    for h in range(heads):
        wo_copy(h).start()

    rows = jnp.concatenate([near_ref[...], far_ref[...]], axis=0)
    mixed = []
    for t in range(parts):
        acc = None
        for k in range(CUT):
            wq_copy(t, k).wait()
            term = jnp.dot(
                rows[:, k * slab : (k + 1) * slab], wq[t, k * slab : (k + 1) * slab], preferred_element_type=jnp.float32
            )
            acc = term if acc is None else acc + term
        mixed.append(acc.astype(jnp.bfloat16))

    row, col = iotas((count, count))
    block = col >> 3
    owner = hid_ref[0] ^ (((block & 1) << 2) | (block & 2) | (block >> 2))
    pick = (((col >> 2) & 1) == row // here) & (owner == ((row % here) >> 2)) & ((col & 3) == (row & 3))
    pick = jnp.where(pick, 1.0, 0.0).astype(jnp.bfloat16)
    ordered = [jnp.dot(pick, part, preferred_element_type=jnp.float32) for part in mixed]
    _, lane = iotas((count, LANES))
    even = lane % 2 == 0
    cosine, sine = turn_ref[0], turn_ref[1]

    def turned(values, h):
        head = values[:, h * HEAD_DIM : h * HEAD_DIM + LANES]
        other = jnp.where(even, pltpu.roll(head, LANES - 1, 1), pltpu.roll(head, 1, 1))
        rest = values[:, h * HEAD_DIM + LANES : (h + 1) * HEAD_DIM]
        return jnp.concatenate([head * cosine + other * sine, rest], axis=1).astype(jnp.bfloat16)

    queries = [turned(ordered[0], h) for h in range(heads)]
    new_keys = [turned(ordered[1], h) for h in range(heads)]
    new_values = ordered[2].astype(jnp.bfloat16)
    scale = HEAD_DIM ** (-0.5)
    line, at = iotas((here, prompt_len))
    tail_line, tail_at = iotas((here, samples * tail_len))
    fresh_line, fresh_at = iotas((here, here))
    fresh_keep = (fresh_at // fresh == fresh_line // fresh) & (fresh_at <= fresh_line)
    sample, _ = iotas((here, 1))
    attended = [[None] * requests for _ in range(heads)]
    for r in range(requests):
        lengths = jnp.zeros((here, 1), jnp.int32)
        for s in range(samples):
            lengths = jnp.where(sample // fresh == s, tlen_ref[r, s], lengths)
        keep = at < plen_ref[r]
        tail_keep = (tail_at // tail_len == tail_line // fresh) & (tail_at % tail_len < lengths)
        own = slice(r * here, (r + 1) * here)
        for i in range(2):
            cache_copy(r, i).wait()
        weighted = []
        for h in range(heads):
            cols = slice(h * HEAD_DIM, (h + 1) * HEAD_DIM)
            query = queries[h][own]
            def scores(keys):
                return lax.dot_general(query, keys, (((1,), (1,)), ((), ())), preferred_element_type=jnp.float32) * scale
            prompt = jnp.where(keep, scores(pk[r, :, cols]), VERY_LOW)
            tail = jnp.where(tail_keep, scores(tk[r, :, cols]), VERY_LOW)
            new = jnp.where(fresh_keep, scores(new_keys[h][own]), VERY_LOW)
            top = jnp.maximum(
                jnp.max(prompt, axis=1, keepdims=True),
                jnp.maximum(jnp.max(tail, axis=1, keepdims=True), jnp.max(new, axis=1, keepdims=True)),
            )
            weights = [jnp.exp(part - top) for part in (prompt, tail, new)]
            total = sum(jnp.sum(part, axis=1, keepdims=True) for part in weights)
            weighted.append(([part.astype(jnp.bfloat16) for part in weights], total))
        for i in range(2, 4):
            cache_copy(r, i).wait()
        for h in range(heads):
            cols = slice(h * HEAD_DIM, (h + 1) * HEAD_DIM)
            weights, total = weighted[h]
            summed = jnp.dot(weights[0], pv[r, :, cols], preferred_element_type=jnp.float32)
            summed = summed + jnp.dot(weights[1], tv[r, :, cols], preferred_element_type=jnp.float32)
            summed = summed + jnp.dot(weights[2], new_values[own, cols], preferred_element_type=jnp.float32)
            attended[h][r] = (summed / total).astype(jnp.bfloat16)
    joined = jnp.concatenate([jnp.concatenate(part, axis=0) for part in attended], axis=1)
    placed = lax.dot_general(pick, joined, (((0,), (0,)), ((), ())), preferred_element_type=jnp.float32).astype(jnp.bfloat16)
    for h in range(heads):
        wo_copy(h).wait()
    out_ref[...] = jnp.dot(placed, wo[...], preferred_element_type=jnp.float32).astype(jnp.bfloat16)


def mixer_call(plen, tlen, hid, near, far, turn, wq, pk, pv, tk, tv, wo):
    parts, width, columns = wq.shape
    requests, prompt_len, _ = pk.shape
    count = near.shape[0] + far.shape[0]
    keys = prompt_len + tk.shape[1]
    return pl.pallas_call(
        mixer_body,
        out_shape=jax.ShapeDtypeStruct((count, width), jnp.bfloat16),
        in_specs=[SMEM] * 3 + [VMEM] * 3 + [HBM] * 6,
        out_specs=VMEM,
        scratch_shapes=[pltpu.VMEM(a.shape, jnp.bfloat16) for a in (wq, pk, pv, tk, tv, wo)]
        + [
            pltpu.SemaphoreType.DMA((parts, CUT)),
            pltpu.SemaphoreType.DMA((requests, 4)),
            pltpu.SemaphoreType.DMA((columns // HEAD_DIM,)),
        ],
        compiler_params=pltpu.CompilerParams(vmem_limit_bytes=60 * MIB),
        cost_estimate=pl.CostEstimate(
            flops=2 * count * columns * (parts * width + 2 * keys + width),
            bytes_accessed=2 * columns * (parts * width + 2 * requests * keys + width),
            transcendentals=count * keys * (columns // HEAD_DIM),
        ),
        name="mixer",
    )(plen, tlen, hid, near, far, turn, wq, pk, pv, tk, tv, wo)


def mlp_body(place_ref, own_ref, other_hbm, near_hbm, far_hbm, *refs):
    packed, (out_own, out_other) = refs[:4], refs[4:6]
    other_ref, near_ref, far_ref, ups, downs, row_sem, up_sem, down_sem = refs[6:]
    row_copies = [
        pltpu.make_async_copy(source, target, row_sem.at[i])
        for i, (source, target) in enumerate(((other_hbm, other_ref), (near_hbm, near_ref), (far_hbm, far_ref)))
    ]
    row_copies[0].start()
    blocks = ups.shape[0]
    def up_copy(p):
        return pltpu.make_async_copy(
            packed[p].at[pl.ds(0, blocks)], ups.at[:, :, pl.ds(p * LANES, LANES)], up_sem.at[p]
        )
    def down_copy(p):
        return pltpu.make_async_copy(
            packed[p].at[pl.ds(blocks, blocks)], downs.at[:, pl.ds(p * LANES, LANES), :], down_sem.at[p]
        )
    for p in range(4):
        up_copy(p).start()
    for p in range(4):
        down_copy(p).start()
    row_copies[1].start()
    row_copies[2].start()
    row_copies[0].wait()
    rows = jnp.concatenate([own_ref[...], other_ref[...]], axis=0)
    units = ups.shape[2]
    for p in range(4):
        up_copy(p).wait()
    hidden = jnp.dot(rows, ups[...].reshape(blocks * LANES, units), preferred_element_type=jnp.float32)
    hidden = jax.nn.gelu(hidden, approximate=True).astype(jnp.bfloat16)
    for p in range(4):
        down_copy(p).wait()
    half = own_ref.shape[0]
    for j in range(0, blocks, 2):
        result = jnp.dot(
            hidden, jnp.concatenate([downs[j], downs[j + 1]], axis=1), preferred_element_type=jnp.float32
        ).astype(jnp.bfloat16)
        cols = slice(j * LANES, (j + 2) * LANES)
        out_own[:, cols] = result[:half]
        out_other[:, cols] = result[half:]
    row_copies[1].wait()
    row_copies[2].wait()
    count = near_ref.shape[0] // 2
    for i in range(2):
        at = pl.ds(pl.multiple_of((place_ref[0] ^ i) * count, count), count)
        part = pl.ds(i * count, count)
        out_own[at] = (
            out_own[at].astype(jnp.float32)
            + near_ref[part].astype(jnp.float32)
            + far_ref[part].astype(jnp.float32)
        ).astype(jnp.bfloat16)


def mlp_call(place, own, other, near, far, packed):
    count, width = own.shape
    units = 4 * LANES
    blocks = width // LANES
    return pl.pallas_call(
        mlp_body,
        out_shape=[jax.ShapeDtypeStruct((count, width), jnp.bfloat16)] * 2,
        in_specs=[SMEM, VMEM] + [HBM] * 7,
        out_specs=[VMEM] * 2,
        scratch_shapes=[
            pltpu.VMEM(other.shape, jnp.bfloat16),
            pltpu.VMEM(near.shape, jnp.bfloat16),
            pltpu.VMEM(far.shape, jnp.bfloat16),
            pltpu.VMEM((blocks, LANES, units), jnp.bfloat16),
            pltpu.VMEM((blocks, units, LANES), jnp.bfloat16),
            pltpu.SemaphoreType.DMA((3,)),
            pltpu.SemaphoreType.DMA((4,)),
            pltpu.SemaphoreType.DMA((4,)),
        ],
        compiler_params=pltpu.CompilerParams(vmem_limit_bytes=24 * MIB),
        cost_estimate=pl.CostEstimate(
            flops=8 * count * width * units,
            bytes_accessed=2 * (4 * count * width + 2 * units * width),
            transcendentals=2 * count * units,
        ),
        name="mlp",
    )(place, own, other, near, far, *packed)


def add_body(a_ref, b_ref, out_ref):
    out_ref[...] = (a_ref[...].astype(jnp.float32) + b_ref[...].astype(jnp.float32)).astype(jnp.bfloat16)


def add_call(a, b):
    return pl.pallas_call(
        add_body,
        out_shape=jax.ShapeDtypeStruct(b.shape, jnp.bfloat16),
        in_specs=[VMEM] * 2,
        out_specs=VMEM,
        compiler_params=pltpu.CompilerParams(vmem_limit_bytes=8 * MIB),
        name="add",
    )(a, b)


def end_body(tokens_ref, returned_ref, gain_ref, score_ref, next_ref, out_ref, rows):
    requests, samples, fresh, width = tokens_ref.shape
    for r in range(requests):
        for s in range(samples):
            at = (r * samples + s) * fresh
            rows[at : at + fresh] = tokens_ref[r, s].astype(jnp.float32)
    added = returned_ref[0].astype(jnp.float32)
    for i in range(1, returned_ref.shape[0]):
        added = added + returned_ref[i].astype(jnp.float32)
    final = rows[...] + added
    scores = jnp.sum(
        normalised(final, gain_ref[...]) * score_ref[...].astype(jnp.float32), axis=1, keepdims=True
    )
    rows[...] = final
    row, col = iotas((final.shape[0], fresh))
    for r in range(requests):
        for s in range(samples):
            at = (r * samples + s) * fresh
            next_ref[r, s] = rows[at : at + fresh].astype(jnp.bfloat16)
            out_ref[r, s : s + 1] = jnp.sum(jnp.where(row == at + col, scores, 0.0), axis=0, keepdims=True)


def end_call(tokens, returned, gain, score_weight):
    width = tokens.shape[-1]
    return pl.pallas_call(
        end_body,
        out_shape=[
            jax.ShapeDtypeStruct(tokens.shape, jnp.bfloat16),
            jax.ShapeDtypeStruct(tokens.shape[:-1], jnp.float32),
        ],
        in_specs=[VMEM] * 4,
        out_specs=[VMEM] * 2,
        scratch_shapes=[pltpu.VMEM((returned.shape[1], width), jnp.float32)],
        compiler_params=pltpu.CompilerParams(vmem_limit_bytes=8 * MIB),
        name="end",
    )(tokens, returned, gain.reshape(1, width), score_weight.reshape(1, width))


def rotation_tables(positions):
    lane = jnp.arange(LANES, dtype=jnp.int32)
    frequency = 10000.0 ** (-((lane // 2).astype(jnp.float32) * (2.0 / ROT)))
    angles = positions.astype(jnp.float32)[:, None] * frequency
    sign = jnp.where(lane % 2 == 0, -1.0, 1.0)
    rotated = lane < ROT
    return jnp.stack(
        [jnp.where(rotated, jnp.cos(angles), 1.0), jnp.where(rotated, jnp.sin(angles) * sign, 0.0)]
    )


def shards(
    tokens,
    input_gain,
    qkv_weight,
    out_weight,
    in_weight,
    down_weight,
    final_gain,
    score_weight,
    prompt_keys,
    prompt_values,
    tail_keys,
    tail_values,
    prompt_lengths,
    tail_lengths,
):
    req_dev, samp_dev, fresh, width = tokens.shape
    own_rows = req_dev * samp_dev * fresh
    groups = token_groups()
    sharing = len(groups[0])
    normed, copies, own_weights = start_call(tokens, input_gain, in_weight, down_weight, sharing)

    near = jnp.concatenate([normed, swap(normed, "u"), swap(normed, "w"), swap(normed, "u", "w")], axis=0)
    near, late_weights = lax.optimization_barrier((near, own_weights))
    far = swap(near, "c")
    packed = [own_weights] + [from_neighbour(late_weights, axis) for axis in "xyz"]

    def exchange(values):
        return lax.all_to_all(values, AXES, 0, 0, axis_index_groups=groups, tiled=True)

    visitors = exchange(copies).reshape(sharing * own_rows, width)
    positions = (
        prompt_lengths[:, None, None]
        + tail_lengths[:, :, None]
        + jnp.arange(fresh, dtype=jnp.int32)[None, None, :]
    )
    slab = tail_keys.shape[-1]
    partial = mixer_call(
        prompt_lengths,
        tail_lengths,
        lax.axis_index(HID).astype(jnp.int32).reshape(1),
        near,
        far,
        rotation_tables(positions.reshape(-1)),
        jnp.transpose(qkv_weight, (1, 0, 2)),
        prompt_keys,
        prompt_values,
        tail_keys.reshape(req_dev, -1, slab),
        tail_values.reshape(req_dev, -1, slab),
        out_weight,
    )
    other_visitors = swap(visitors, "c")
    half = partial.shape[0] // 2
    projected = add_call(partial[:half], swap(partial[half:], "c"))
    half = projected.shape[0] // 2
    projected_far = swap(projected[half:], "w")
    projected, projected_far, packed, visitors, other_visitors = lax.optimization_barrier(
        (projected, projected_far, packed, visitors, other_visitors)
    )

    place = lax.axis_index("y") * SIDE + lax.axis_index("x") // 2 * 2 + lax.axis_index("u")
    place = place.astype(jnp.int32).reshape(1)
    mine, others = mlp_call(place, visitors, other_visitors, projected[:half], projected_far, packed)
    summed = add_call(mine, swap(others, "c"))
    returned = exchange(summed.reshape(sharing, own_rows, width))
    next_hidden, sample_scores = end_call(tokens, returned, final_gain, score_weight)
    return (next_hidden, sample_scores)


def solution(mesh):
    grid = Mesh(mesh.devices.reshape(SIDE, SIDE, 2, 2, CORES), AXES)
    placed = (
        P(REQ, HID, None, None),
        P(),
        P(None, None, HID),
        P(HID, None),
        P(None, REQ + HID),
        P(REQ + HID, None),
        P(),
        P(),
        P(REQ, None, HID),
        P(REQ, None, HID),
        P(REQ, None, None, HID),
        P(REQ, None, None, HID),
        P(REQ),
        P(REQ, None),
    )
    return jax.shard_map(
        shards,
        mesh=grid,
        in_specs=placed,
        out_specs=(P(REQ, HID, None, None), P(REQ, HID, None)),
        check_vma=False,
    )
```

```python
import jax
import jax.numpy as jnp
from jax import lax
from jax.experimental import pallas as pl
from jax.experimental.pallas import tpu as pltpu
from jax.sharding import Mesh
from jax.sharding import PartitionSpec as P

HEAD_DIM = 256
ROT = 64
LANES = 128
VERY_LOW = -1e30
CUT = 2
SUM_BLOCKS = 4
MIB = 2**20
SMEM = pl.BlockSpec(memory_space=pltpu.SMEM)
VMEM = pl.BlockSpec(memory_space=pltpu.VMEM)
HBM = pl.BlockSpec(memory_space=pltpu.HBM)
SIDE = 4
CORES = 2
AXES = ("y", "x", "u", "w", "c")
REQ = ("y", "x")
HID = ("u", "w", "c")


def device_at(y, x, z, core):
    return (((y % SIDE) * SIDE + x % SIDE) * SIDE + z % SIDE) * CORES + core


def places():
    for y in range(SIDE):
        for x in range(SIDE):
            for z in range(SIDE):
                for core in range(CORES):
                    yield y, x, z, core


def token_groups():
    groups = {}
    for y, x, z, core in places():
        groups.setdefault(((x + z) % 2, (y + z) % 2, core), []).append(device_at(y, x, z, core))
    return [sorted(group) for group in groups.values()]


def from_neighbour(values, axis):
    moves = []
    for y, x, z, core in places():
        step = 1 - 2 * core
        target = device_at(
            y + step * (axis == "y"), x + step * (axis == "x"), z + step * (axis == "z"), core
        )
        moves.append((device_at(y, x, z, core), target))
    return lax.ppermute(values, AXES, moves)


def swap(values, *axes):
    last = 2 ** len(axes) - 1
    return lax.ppermute(values, axes, [(i, last - i) for i in range(last + 1)])


def normalised(values, gain):
    centred = values - jnp.mean(values, axis=1, keepdims=True)
    spread = jnp.mean(centred * centred, axis=1, keepdims=True)
    return centred * lax.rsqrt(spread + 1e-05) * gain


def start_body(
    tokens_hbm, gain_hbm, up_hbm, down_hbm, normed_ref, copies_hbm, packed_hbm, tokens_ref, gain_ref, rows, packed, down_ref, sem, out_sem, copy_sem
):
    requests, samples, fresh, width = tokens_ref.shape
    blocks = up_hbm.shape[0]
    upper, lower = pl.ds(0, blocks), pl.ds(blocks, blocks)
    inward = [
        pltpu.make_async_copy(tokens_hbm, tokens_ref, sem.at[0]),
        pltpu.make_async_copy(gain_hbm, gain_ref, sem.at[1]),
        pltpu.make_async_copy(down_hbm, down_ref, sem.at[2]),
        pltpu.make_async_copy(up_hbm, packed.at[upper], sem.at[3]),
    ]
    outward = [
        pltpu.make_async_copy(packed.at[lower], packed_hbm.at[lower], out_sem.at[0]),
        pltpu.make_async_copy(packed.at[upper], packed_hbm.at[upper], out_sem.at[1]),
    ]
    copies = [
        pltpu.make_async_copy(normed_ref, copies_hbm.at[i], copy_sem.at[i]) for i in range(copies_hbm.shape[0])
    ]
    for copy in inward:
        copy.start()
    inward[0].wait()
    inward[1].wait()
    for r in range(requests):
        for s in range(samples):
            at = (r * samples + s) * fresh
            rows[at : at + fresh] = tokens_ref[r, s].astype(jnp.float32)
    normed_ref[...] = normalised(rows[...], gain_ref[...]).astype(jnp.bfloat16)
    for copy in copies:
        copy.start()
    inward[2].wait()
    for j in range(blocks):
        packed[blocks + j] = down_ref[:, j * LANES : (j + 1) * LANES]
    outward[0].start()
    inward[3].wait()
    outward[1].start()
    for copy in outward + copies:
        copy.wait()


def start_call(tokens, gain, up, down, sharing):
    requests, samples, fresh, width = tokens.shape
    own_rows = requests * samples * fresh
    blocks = width // LANES
    return pl.pallas_call(
        start_body,
        out_shape=[
            jax.ShapeDtypeStruct((own_rows, width), jnp.bfloat16),
            jax.ShapeDtypeStruct((sharing, own_rows, width), jnp.bfloat16),
            jax.ShapeDtypeStruct((2 * blocks, LANES, LANES), jnp.bfloat16),
        ],
        in_specs=[HBM] * 4,
        out_specs=[VMEM, HBM, HBM],
        scratch_shapes=[
            pltpu.VMEM(tokens.shape, jnp.bfloat16),
            pltpu.VMEM((1, width), jnp.float32),
            pltpu.VMEM((own_rows, width), jnp.float32),
            pltpu.VMEM((2 * blocks, LANES, LANES), jnp.bfloat16),
            pltpu.VMEM(down.shape, jnp.bfloat16),
            pltpu.SemaphoreType.DMA((4,)),
            pltpu.SemaphoreType.DMA((2,)),
            pltpu.SemaphoreType.DMA((sharing,)),
        ],
        compiler_params=pltpu.CompilerParams(vmem_limit_bytes=60 * MIB),
        name="start",
    )(tokens, gain.reshape(1, width), up.reshape(blocks, LANES, LANES), down)


def iotas(shape):
    return lax.broadcasted_iota(jnp.int32, shape, 0), lax.broadcasted_iota(jnp.int32, shape, 1)

def mixer_body(
    plen_ref, tlen_ref, hid_ref, near_ref, far_ref, turn_ref, wq_hbm, pk_hbm, pv_hbm, tk_hbm, tv_hbm, wo_hbm,
    out_ref, wq, pk, pv, tk, tv, wo, wq_sem, cache_sem, wo_sem
):
    parts, width, columns = wq.shape
    requests, prompt_len, _ = pk.shape
    samples = tlen_ref.shape[1]
    tail_len = tk.shape[1] // samples
    count = near_ref.shape[0] + far_ref.shape[0]
    here = count // requests
    fresh = here // samples
    heads = columns // HEAD_DIM
    slab = width // CUT
    def wq_copy(t, k):
        rows = pl.ds(k * slab, slab)
        return pltpu.make_async_copy(wq_hbm.at[t, rows], wq.at[t, rows], wq_sem.at[t, k])
    caches = ((pk_hbm, pk), (tk_hbm, tk), (pv_hbm, pv), (tv_hbm, tv))
    def cache_copy(r, i):
        source, target = caches[i]
        return pltpu.make_async_copy(source.at[r], target.at[r], cache_sem.at[r, i])
    def wo_copy(h):
        rows = pl.ds(h * HEAD_DIM, HEAD_DIM)
        return pltpu.make_async_copy(wo_hbm.at[rows], wo.at[rows], wo_sem.at[h])
    for t in range(parts):
        for k in range(CUT):
            wq_copy(t, k).start()
    for r in range(requests):
        for i in range(len(caches)):
            cache_copy(r, i).start()
    for h in range(heads):
        wo_copy(h).start()

    rows = jnp.concatenate([near_ref[...], far_ref[...]], axis=0)
    mixed = []
    for t in range(parts):
        acc = None
        for k in range(CUT):
            wq_copy(t, k).wait()
            term = jnp.dot(
                rows[:, k * slab : (k + 1) * slab], wq[t, k * slab : (k + 1) * slab], preferred_element_type=jnp.float32
            )
            acc = term if acc is None else acc + term
        mixed.append(acc.astype(jnp.bfloat16))

    row, col = iotas((count, count))
    block = col >> 3
    owner = hid_ref[0] ^ (((block & 1) << 2) | (block & 2) | (block >> 2))
    pick = (((col >> 2) & 1) == row // here) & (owner == ((row % here) >> 2)) & ((col & 3) == (row & 3))
    pick = jnp.where(pick, 1.0, 0.0).astype(jnp.bfloat16)
    ordered = [jnp.dot(pick, part, preferred_element_type=jnp.float32) for part in mixed]
    _, lane = iotas((count, LANES))
    even = lane % 2 == 0
    cosine, sine = turn_ref[0], turn_ref[1]

    def turned(values, h):
        head = values[:, h * HEAD_DIM : h * HEAD_DIM + LANES]
        other = jnp.where(even, pltpu.roll(head, LANES - 1, 1), pltpu.roll(head, 1, 1))
        rest = values[:, h * HEAD_DIM + LANES : (h + 1) * HEAD_DIM]
        return jnp.concatenate([head * cosine + other * sine, rest], axis=1).astype(jnp.bfloat16)

    queries = [turned(ordered[0], h) for h in range(heads)]
    new_keys = [turned(ordered[1], h) for h in range(heads)]
    new_values = ordered[2].astype(jnp.bfloat16)
    scale = HEAD_DIM ** (-0.5)
    line, at = iotas((here, prompt_len))
    tail_line, tail_at = iotas((here, samples * tail_len))
    fresh_line, fresh_at = iotas((here, here))
    fresh_keep = (fresh_at // fresh == fresh_line // fresh) & (fresh_at <= fresh_line)
    sample, _ = iotas((here, 1))
    attended = [[None] * requests for _ in range(heads)]
    for r in range(requests):
        lengths = jnp.zeros((here, 1), jnp.int32)
        for s in range(samples):
            lengths = jnp.where(sample // fresh == s, tlen_ref[r, s], lengths)
        keep = at < plen_ref[r]
        tail_keep = (tail_at // tail_len == tail_line // fresh) & (tail_at % tail_len < lengths)
        own = slice(r * here, (r + 1) * here)
        for i in range(2):
            cache_copy(r, i).wait()
        weighted = []
        for h in range(heads):
            cols = slice(h * HEAD_DIM, (h + 1) * HEAD_DIM)
            query = queries[h][own]
            def scores(keys):
                return lax.dot_general(query, keys, (((1,), (1,)), ((), ())), preferred_element_type=jnp.float32) * scale
            prompt = jnp.where(keep, scores(pk[r, :, cols]), VERY_LOW)
            tail = jnp.where(tail_keep, scores(tk[r, :, cols]), VERY_LOW)
            new = jnp.where(fresh_keep, scores(new_keys[h][own]), VERY_LOW)
            top = jnp.maximum(
                jnp.max(prompt, axis=1, keepdims=True),
                jnp.maximum(jnp.max(tail, axis=1, keepdims=True), jnp.max(new, axis=1, keepdims=True)),
            )
            weights = [jnp.exp(part - top) for part in (prompt, tail, new)]
            total = sum(jnp.sum(part, axis=1, keepdims=True) for part in weights)
            weighted.append(([part.astype(jnp.bfloat16) for part in weights], total))
        for i in range(2, 4):
            cache_copy(r, i).wait()
        for h in range(heads):
            cols = slice(h * HEAD_DIM, (h + 1) * HEAD_DIM)
            weights, total = weighted[h]
            summed = jnp.dot(weights[0], pv[r, :, cols], preferred_element_type=jnp.float32)
            summed = summed + jnp.dot(weights[1], tv[r, :, cols], preferred_element_type=jnp.float32)
            summed = summed + jnp.dot(weights[2], new_values[own, cols], preferred_element_type=jnp.float32)
            attended[h][r] = (summed / total).astype(jnp.bfloat16)
    joined = jnp.concatenate([jnp.concatenate(part, axis=0) for part in attended], axis=1)
    placed = lax.dot_general(pick, joined, (((0,), (0,)), ((), ())), preferred_element_type=jnp.float32).astype(jnp.bfloat16)
    for h in range(heads):
        wo_copy(h).wait()
    out_ref[...] = jnp.dot(placed, wo[...], preferred_element_type=jnp.float32).astype(jnp.bfloat16)


def mixer_call(plen, tlen, hid, near, far, turn, wq, pk, pv, tk, tv, wo):
    parts, width, columns = wq.shape
    requests, prompt_len, _ = pk.shape
    count = near.shape[0] + far.shape[0]
    keys = prompt_len + tk.shape[1]
    return pl.pallas_call(
        mixer_body,
        out_shape=jax.ShapeDtypeStruct((count, width), jnp.bfloat16),
        in_specs=[SMEM] * 3 + [VMEM] * 3 + [HBM] * 6,
        out_specs=VMEM,
        scratch_shapes=[pltpu.VMEM(a.shape, jnp.bfloat16) for a in (wq, pk, pv, tk, tv, wo)]
        + [
            pltpu.SemaphoreType.DMA((parts, CUT)),
            pltpu.SemaphoreType.DMA((requests, 4)),
            pltpu.SemaphoreType.DMA((columns // HEAD_DIM,)),
        ],
        compiler_params=pltpu.CompilerParams(vmem_limit_bytes=60 * MIB),
        cost_estimate=pl.CostEstimate(
            flops=2 * count * columns * (parts * width + 2 * keys + width),
            bytes_accessed=2 * columns * (parts * width + 2 * requests * keys + width),
            transcendentals=count * keys * (columns // HEAD_DIM),
        ),
        name="mixer",
    )(plen, tlen, hid, near, far, turn, wq, pk, pv, tk, tv, wo)


def mlp_body(place_ref, own_ref, other_hbm, near_hbm, far_hbm, *refs):
    packed, (out_own, out_other) = refs[:4], refs[4:6]
    other_ref, near_ref, far_ref, ups, downs, row_sem, up_sem, down_sem = refs[6:]
    row_copies = [
        pltpu.make_async_copy(source, target, row_sem.at[i])
        for i, (source, target) in enumerate(((other_hbm, other_ref), (near_hbm, near_ref), (far_hbm, far_ref)))
    ]
    row_copies[0].start()
    blocks = ups.shape[0]
    def up_copy(p):
        return pltpu.make_async_copy(
            packed[p].at[pl.ds(0, blocks)], ups.at[:, :, pl.ds(p * LANES, LANES)], up_sem.at[p]
        )
    def down_copy(p):
        return pltpu.make_async_copy(
            packed[p].at[pl.ds(blocks, blocks)], downs.at[:, pl.ds(p * LANES, LANES), :], down_sem.at[p]
        )
    for p in range(4):
        up_copy(p).start()
    for p in range(4):
        down_copy(p).start()
    row_copies[1].start()
    row_copies[2].start()
    row_copies[0].wait()
    rows = jnp.concatenate([own_ref[...], other_ref[...]], axis=0)
    units = ups.shape[2]
    for p in range(4):
        up_copy(p).wait()
    hidden = jnp.dot(rows, ups[...].reshape(blocks * LANES, units), preferred_element_type=jnp.float32)
    hidden = jax.nn.gelu(hidden, approximate=True).astype(jnp.bfloat16)
    for p in range(4):
        down_copy(p).wait()
    half = own_ref.shape[0]
    for j in range(0, blocks, 2):
        result = jnp.dot(
            hidden, jnp.concatenate([downs[j], downs[j + 1]], axis=1), preferred_element_type=jnp.float32
        ).astype(jnp.bfloat16)
        cols = slice(j * LANES, (j + 2) * LANES)
        out_own[:, cols] = result[:half]
        out_other[:, cols] = result[half:]
    row_copies[1].wait()
    row_copies[2].wait()
    count = near_ref.shape[0] // 2
    for i in range(2):
        at = pl.ds(pl.multiple_of((place_ref[0] ^ i) * count, count), count)
        part = pl.ds(i * count, count)
        out_own[at] = (
            out_own[at].astype(jnp.float32)
            + near_ref[part].astype(jnp.float32)
            + far_ref[part].astype(jnp.float32)
        ).astype(jnp.bfloat16)


def mlp_call(place, own, other, near, far, packed):
    count, width = own.shape
    units = 4 * LANES
    blocks = width // LANES
    return pl.pallas_call(
        mlp_body,
        out_shape=[jax.ShapeDtypeStruct((count, width), jnp.bfloat16)] * 2,
        in_specs=[SMEM, VMEM] + [HBM] * 7,
        out_specs=[VMEM] * 2,
        scratch_shapes=[
            pltpu.VMEM(other.shape, jnp.bfloat16),
            pltpu.VMEM(near.shape, jnp.bfloat16),
            pltpu.VMEM(far.shape, jnp.bfloat16),
            pltpu.VMEM((blocks, LANES, units), jnp.bfloat16),
            pltpu.VMEM((blocks, units, LANES), jnp.bfloat16),
            pltpu.SemaphoreType.DMA((3,)),
            pltpu.SemaphoreType.DMA((4,)),
            pltpu.SemaphoreType.DMA((4,)),
        ],
        compiler_params=pltpu.CompilerParams(vmem_limit_bytes=24 * MIB),
        cost_estimate=pl.CostEstimate(
            flops=8 * count * width * units,
            bytes_accessed=2 * (4 * count * width + 2 * units * width),
            transcendentals=2 * count * units,
        ),
        name="mlp",
    )(place, own, other, near, far, *packed)


def add_body(a_ref, b_ref, out_ref):
    out_ref[...] = (a_ref[...].astype(jnp.float32) + b_ref[...].astype(jnp.float32)).astype(jnp.bfloat16)


def add_call(a, b):
    return pl.pallas_call(
        add_body,
        out_shape=jax.ShapeDtypeStruct(b.shape, jnp.bfloat16),
        in_specs=[VMEM] * 2,
        out_specs=VMEM,
        compiler_params=pltpu.CompilerParams(vmem_limit_bytes=8 * MIB),
        name="add",
    )(a, b)


def sum_body(a_ref, b_ref, out_hbm, total, sem):
    step = total.shape[0] // SUM_BLOCKS
    copies = []
    for i in range(SUM_BLOCKS):
        at = pl.ds(i * step, step)
        total[at] = (a_ref[at].astype(jnp.float32) + b_ref[at].astype(jnp.float32)).astype(jnp.bfloat16)
        copies.append(pltpu.make_async_copy(total.at[at], out_hbm.at[at], sem.at[i]))
        copies[i].start()
    for copy in copies:
        copy.wait()


def sum_call(a, b):
    return pl.pallas_call(
        sum_body,
        out_shape=jax.ShapeDtypeStruct(b.shape, jnp.bfloat16),
        in_specs=[VMEM] * 2,
        out_specs=HBM,
        scratch_shapes=[pltpu.VMEM(b.shape, jnp.bfloat16), pltpu.SemaphoreType.DMA((SUM_BLOCKS,))],
        compiler_params=pltpu.CompilerParams(vmem_limit_bytes=8 * MIB),
        name="sum",
    )(a, b)


def end_body(tokens_ref, returned_ref, gain_ref, score_ref, next_ref, out_ref, rows):
    requests, samples, fresh, width = tokens_ref.shape
    for r in range(requests):
        for s in range(samples):
            at = (r * samples + s) * fresh
            rows[at : at + fresh] = tokens_ref[r, s].astype(jnp.float32)
    added = returned_ref[0].astype(jnp.float32)
    for i in range(1, returned_ref.shape[0]):
        added = added + returned_ref[i].astype(jnp.float32)
    final = rows[...] + added
    scores = jnp.sum(
        normalised(final, gain_ref[...]) * score_ref[...].astype(jnp.float32), axis=1, keepdims=True
    )
    rows[...] = final
    row, col = iotas((final.shape[0], fresh))
    for r in range(requests):
        for s in range(samples):
            at = (r * samples + s) * fresh
            next_ref[r, s] = rows[at : at + fresh].astype(jnp.bfloat16)
            out_ref[r, s : s + 1] = jnp.sum(jnp.where(row == at + col, scores, 0.0), axis=0, keepdims=True)


def end_call(tokens, returned, gain, score_weight):
    width = tokens.shape[-1]
    return pl.pallas_call(
        end_body,
        out_shape=[
            jax.ShapeDtypeStruct(tokens.shape, jnp.bfloat16),
            jax.ShapeDtypeStruct(tokens.shape[:-1], jnp.float32),
        ],
        in_specs=[VMEM] * 4,
        out_specs=[VMEM] * 2,
        scratch_shapes=[pltpu.VMEM((returned.shape[1], width), jnp.float32)],
        compiler_params=pltpu.CompilerParams(vmem_limit_bytes=8 * MIB),
        name="end",
    )(tokens, returned, gain.reshape(1, width), score_weight.reshape(1, width))


def rotation_tables(positions):
    lane = jnp.arange(LANES, dtype=jnp.int32)
    frequency = 10000.0 ** (-((lane // 2).astype(jnp.float32) * (2.0 / ROT)))
    angles = positions.astype(jnp.float32)[:, None] * frequency
    sign = jnp.where(lane % 2 == 0, -1.0, 1.0)
    rotated = lane < ROT
    return jnp.stack(
        [jnp.where(rotated, jnp.cos(angles), 1.0), jnp.where(rotated, jnp.sin(angles) * sign, 0.0)]
    )


def shards(
    tokens,
    input_gain,
    qkv_weight,
    out_weight,
    in_weight,
    down_weight,
    final_gain,
    score_weight,
    prompt_keys,
    prompt_values,
    tail_keys,
    tail_values,
    prompt_lengths,
    tail_lengths,
):
    req_dev, samp_dev, fresh, width = tokens.shape
    own_rows = req_dev * samp_dev * fresh
    groups = token_groups()
    sharing = len(groups[0])
    normed, copies, own_weights = start_call(tokens, input_gain, in_weight, down_weight, sharing)

    near = jnp.concatenate([normed, swap(normed, "u"), swap(normed, "w"), swap(normed, "u", "w")], axis=0)
    near, late_weights = lax.optimization_barrier((near, own_weights))
    far = swap(near, "c")
    packed = [own_weights] + [from_neighbour(late_weights, axis) for axis in "xyz"]

    def exchange(values):
        return lax.all_to_all(values, AXES, 0, 0, axis_index_groups=groups, tiled=True)

    visitors = exchange(copies).reshape(sharing * own_rows, width)
    positions = (
        prompt_lengths[:, None, None]
        + tail_lengths[:, :, None]
        + jnp.arange(fresh, dtype=jnp.int32)[None, None, :]
    )
    slab = tail_keys.shape[-1]
    partial = mixer_call(
        prompt_lengths,
        tail_lengths,
        lax.axis_index(HID).astype(jnp.int32).reshape(1),
        near,
        far,
        rotation_tables(positions.reshape(-1)),
        jnp.transpose(qkv_weight, (1, 0, 2)),
        prompt_keys,
        prompt_values,
        tail_keys.reshape(req_dev, -1, slab),
        tail_values.reshape(req_dev, -1, slab),
        out_weight,
    )
    other_visitors = swap(visitors, "c")
    half = partial.shape[0] // 2
    projected = add_call(partial[:half], swap(partial[half:], "c"))
    half = projected.shape[0] // 2
    projected_far = swap(projected[half:], "w")
    projected, projected_far, packed, visitors, other_visitors = lax.optimization_barrier(
        (projected, projected_far, packed, visitors, other_visitors)
    )

    place = lax.axis_index("y") * SIDE + lax.axis_index("x") // 2 * 2 + lax.axis_index("u")
    place = place.astype(jnp.int32).reshape(1)
    mine, others = mlp_call(place, visitors, other_visitors, projected[:half], projected_far, packed)
    summed = sum_call(mine, swap(others, "c"))
    returned = exchange(summed.reshape(sharing, own_rows, width))
    next_hidden, sample_scores = end_call(tokens, returned, final_gain, score_weight)
    return (next_hidden, sample_scores)


def solution(mesh):
    grid = Mesh(mesh.devices.reshape(SIDE, SIDE, 2, 2, CORES), AXES)
    placed = (
        P(REQ, HID, None, None),
        P(),
        P(None, None, HID),
        P(HID, None),
        P(None, REQ + HID),
        P(REQ + HID, None),
        P(),
        P(),
        P(REQ, None, HID),
        P(REQ, None, HID),
        P(REQ, None, None, HID),
        P(REQ, None, None, HID),
        P(REQ),
        P(REQ, None),
    )
    return jax.shard_map(
        shards,
        mesh=grid,
        in_specs=placed,
        out_specs=(P(REQ, HID, None, None), P(REQ, HID, None)),
        check_vma=False,
    )
```
